32 devices in a mesh: grp: 2 (over y), row: 8 (over z, x), sub: 2 (over core).
Axes of the slice: x: 2, y: 2, z: 4, core: 2. Of those that a mesh axis runs over, the one named last changes fastest.
Arguments:
- right_sides: bfloat16 [32768, 256], P(('grp', 'row', 'sub')), parts along dimension 0, may hold values from -6 to 6
- leaf_inverse: bfloat16 [32768, 512], P(('grp', 'row', 'sub')), parts along dimension 0, may hold values from -0.25 to 0.25
- basis_one: bfloat16 [32768, 256], P(('grp', 'row', 'sub')), parts along dimension 0, may hold values from -1.5 to 1.5
- basis_two: bfloat16 [32768, 256], P(('grp', 'row', 'sub')), parts along dimension 0, may hold values from -1.5 to 1.5
- basis_three: bfloat16 [32768, 256], P(('grp', 'row', 'sub')), parts along dimension 0, may hold values from -1.5 to 1.5
- capacity_one: bfloat16 [1024, 512], P('grp'), parts along dimension 0, may hold values from -0.01171875 to 0.01171875
- capacity_two: bfloat16 [1024, 512], P('grp'), parts along dimension 0, may hold values from -0.005859375 to 0.005859375
- capacity_three: bfloat16 [1024, 512], P('grp'), parts along dimension 0, may hold values from -0.0029296875 to 0.0029296875
Outputs:
- solution: bfloat16 [32768, 256], P(('grp', 'row', 'sub')), parts along dimension 0
The draws below stay inside these ranges and needn't reach their ends.
There are 2 independent parts, one for each index of `grp`. The reference program is written for one: setup_inputs(seed, part) draws one part's arguments, and reference() takes and returns one part's arrays. A program takes and returns all parts, laid end to end along the dimension named above; each array names one. Nothing has to cross between parts.
All inputs are finite; a program needn't handle non-finite values.
Results may differ from the reference program's by a relative error of at most 0.008.
Values sent between devices are 32-bit elements; how exact they have to be, the bound alone decides.
No kernel may reach another device: no remote copies, remote signals or barrier semaphores. Data moves between devices by JAX's collectives and lax.ppermute only.
A program may use at most 64 MiB of HBM per device.

```python
import jax
import jax.numpy as jnp
from jax import lax

LEAF = 512
RANK = 256
RHS = 256
ROWS = 16384
CHILD_TWO = 2048
CHILD_THREE = 8192


def levels(key, extent, shards, least, largest):
    def one(dim, shards_of):
        draws = jax.random.uniform(jax.random.fold_in(jax.random.fold_in(key, 6), dim), (shards_of,), jnp.float32, least / len(shards), largest / len(shards))
        return jnp.repeat(jnp.exp(draws), extent[dim] // shards_of).reshape((-1,) + (1,) * (len(extent) - dim - 1))

    factor_of = one(*shards[0])
    for cut in shards[1:]:
        factor_of = factor_of * one(*cut)
    return factor_of


def noise(key, shape, scale, bound, shards=(), held_as=jnp.bfloat16):
    result = scale * jax.random.normal(key, shape, jnp.float32)
    if shards:
        result = result * levels(key, shape, shards, -0.22, 0.18)
    return jnp.clip(result, -bound, bound).astype(held_as)


def setup_inputs(seed: int = 0, part: int = 0) -> dict:
    keys = jax.random.split(jax.random.key(seed), 9)
    own_keys = jax.random.split(jax.random.fold_in(keys[8], part), 9)
    return {
        "right_sides": noise(own_keys[0], (ROWS, RHS), 1.0, 6.0, ((0, 16),)),
        "leaf_inverse": noise(own_keys[1], (ROWS, LEAF), LEAF ** -0.5, 0.25, ((0, 16),)),
        "basis_one": noise(own_keys[2], (ROWS, RANK), (RANK // 16) ** -0.5, 1.5, ((0, 16),)),
        "basis_two": noise(own_keys[3], (ROWS, RANK), (RANK // 16) ** -0.5, 1.5, ((0, 16),)),
        "basis_three": noise(own_keys[4], (ROWS, RANK), (RANK // 16) ** -0.5, 1.5, ((0, 16),)),
        "capacity_one": noise(own_keys[5], (2 * RANK, 2 * RANK), (2 * RANK * LEAF) ** -0.5, 0.01171875),
        "capacity_two": noise(own_keys[6], (2 * RANK, 2 * RANK), (2 * RANK * CHILD_TWO) ** -0.5, 0.005859375),
        "capacity_three": noise(own_keys[7], (2 * RANK, 2 * RANK), (2 * RANK * CHILD_THREE) ** -0.5, 0.0029296875),
    }


def reference(right_sides, leaf_inverse, basis_one, basis_two, basis_three, capacity_one, capacity_two, capacity_three):
    leaves = ROWS // LEAF
    highest = lax.Precision.HIGHEST
    field = jnp.einsum("lij,ljm->lim", leaf_inverse.astype(jnp.float32).reshape(leaves, LEAF, LEAF), right_sides.astype(jnp.float32).reshape(leaves, LEAF, RHS), precision=highest)
    field = field.reshape(ROWS, RHS)
    for basis, capacity, child in ((basis_one, capacity_one, LEAF), (basis_two, capacity_two, CHILD_TWO), (basis_three, capacity_three, CHILD_THREE)):
        nodes = ROWS // (2 * child)
        blocks = basis.astype(jnp.float32).reshape(nodes, 2, child, RANK)
        rounded = field.astype(jnp.bfloat16).astype(jnp.float32).reshape(nodes, 2, child, RHS)
        stacked = jnp.einsum("ncrk,ncrm->nckm", blocks, rounded, precision=highest).reshape(nodes, 2 * RANK, RHS)
        coefficients = jnp.einsum("ij,njm->nim", capacity.astype(jnp.float32), stacked, precision=highest)
        coefficients = coefficients.astype(jnp.bfloat16).astype(jnp.float32).reshape(nodes, 2, RANK, RHS)
        update = jnp.einsum("ncrk,nckm->ncrm", blocks, coefficients, precision=highest)
        field = field - update.reshape(ROWS, RHS)
    return field.astype(jnp.bfloat16)
```

```python
import jax
import jax.numpy as jnp
from jax import lax
from jax.sharding import PartitionSpec as P


def from_partner(array, axis, stride):
    return lax.ppermute(array, axis, [(i, i ^ 1 << stride) for i in range(lax.axis_size(axis))])


def project(basis, field):
    return jnp.einsum(
        "rk,rm->km", basis, field.astype(jnp.bfloat16), preferred_element_type=jnp.float32
    )


def core_total(projected):
    return projected + from_partner(projected, "sub", 0)


def pair_sum(projected, low_bits):
    for bit_index in range(low_bits):
        projected = projected + from_partner(projected, "row", bit_index)
    sibling_sum = from_partner(projected, "row", low_bits)
    return (projected, sibling_sum)


def pair_stack(own_sum, sibling_sum, child_side):
    first = jnp.where(child_side == 0, own_sum, sibling_sum)
    second = jnp.where(child_side == 0, sibling_sum, own_sum)
    return jnp.concatenate([first, second], axis=0)


def correct(field, basis, capacity, stacked, child_side):
    basis_rank = basis.shape[1]
    own_rows = lax.dynamic_slice_in_dim(capacity, child_side * basis_rank, basis_rank, 0)
    coefficients = jnp.dot(
        own_rows.astype(jnp.float32),
        stacked,
        precision=lax.Precision.HIGHEST,
        preferred_element_type=jnp.float32,
    )
    return field - jnp.dot(
        basis, coefficients.astype(jnp.bfloat16), preferred_element_type=jnp.float32
    )


def per_device(
    right_sides,
    leaf_inverse,
    basis_one,
    basis_two,
    basis_three,
    capacity_one,
    capacity_two,
    capacity_three,
):
    leaf_order = leaf_inverse.shape[1]
    leaves = leaf_inverse.shape[0] // leaf_order
    width_rhs = right_sides.shape[1]
    basis_rank = basis_one.shape[1]
    field = jnp.einsum(
        "lij,ljm->lim",
        leaf_inverse.reshape(leaves, leaf_order, leaf_order),
        right_sides.reshape(leaves, leaf_order, width_rhs),
        preferred_element_type=jnp.float32,
    )
    field = field.reshape(leaves * leaf_order, width_rhs)
    nodes = leaves // 2
    blocks = basis_one.reshape(nodes, 2, leaf_order, basis_rank)
    rounded = field.astype(jnp.bfloat16).reshape(nodes, 2, leaf_order, width_rhs)
    projection = jnp.einsum(
        "ncrk,ncrm->nckm", blocks, rounded, preferred_element_type=jnp.float32
    ).reshape(nodes, 2 * basis_rank, width_rhs)
    coefficients = jnp.einsum(
        "ij,njm->nim",
        capacity_one.astype(jnp.float32),
        projection,
        precision=lax.Precision.HIGHEST,
        preferred_element_type=jnp.float32,
    )
    coefficients = coefficients.astype(jnp.bfloat16).reshape(nodes, 2, basis_rank, width_rhs)
    update = jnp.einsum("ncrk,nckm->ncrm", blocks, coefficients, preferred_element_type=jnp.float32)
    field = field - update.reshape(leaves * leaf_order, width_rhs)
    row_count = lax.axis_size("row")
    row_index = lax.axis_index("row")
    width_two = row_count // 8
    width_three = row_count // 2
    side_two = row_index // width_two % 2
    side_three = row_index // width_three % 2
    own_sum, sibling_sum = pair_sum(
        core_total(project(basis_two, field)), width_two.bit_length() - 1
    )
    field = correct(
        field, basis_two, capacity_two, pair_stack(own_sum, sibling_sum, side_two), side_two
    )
    own_sum, sibling_sum = pair_sum(
        core_total(project(basis_three, field)), width_three.bit_length() - 1
    )
    field = correct(
        field, basis_three, capacity_three, pair_stack(own_sum, sibling_sum, side_three), side_three
    )
    return field.astype(jnp.bfloat16)


def solution(mesh):
    in_specs = (
        P(("grp", "row", "sub"), None),
        P(("grp", "row", "sub"), None),
        P(("grp", "row", "sub"), None),
        P(("grp", "row", "sub"), None),
        P(("grp", "row", "sub"), None),
        P("grp", None),
        P("grp", None),
        P("grp", None),
    )
    out_specs = P(("grp", "row", "sub"), None)
    return jax.shard_map(
        per_device, mesh=mesh, in_specs=in_specs, out_specs=out_specs, check_vma=False
    )
```

```python
import functools

import jax
import jax.numpy as jnp
from jax import lax
from jax.experimental import pallas as pl
from jax.experimental.pallas import tpu as pltpu
from jax.sharding import PartitionSpec as P


F32, BF16 = jnp.float32, jnp.bfloat16
VM = pl.BlockSpec(memory_space=pltpu.VMEM)
HB = pl.BlockSpec(memory_space=pl.ANY)


def nn(a, b):
    return lax.dot_general(a, b, (((1,), (0,)), ((), ())), preferred_element_type=F32)


def nt(a, b):
    return lax.dot_general(a, b, (((1,), (1,)), ((), ())), preferred_element_type=F32)


def tn(a, b):
    return lax.dot_general(a, b, (((0,), (0,)), ((), ())), preferred_element_type=F32)


def split(x, terms):
    parts = []
    for _ in range(terms - 1):
        part = x.astype(BF16)
        parts.append(part)
        x = x - part.astype(F32)
    parts.append(x.astype(BF16))
    return parts


def exact_nt(x, capacity):
    rows = x.shape[0]
    out = nt(jnp.concatenate(split(x, 3), axis=0), capacity)
    return out[:rows] + (out[rows : 2 * rows] + out[2 * rows :])


def partner(array, axis, bit):
    return lax.ppermute(array, axis, [(i, i ^ 1 << bit) for i in range(lax.axis_size(axis))])


def params(kib):
    return pltpu.CompilerParams(vmem_limit_bytes=kib * 1024)


def fetch(pairs, sems):
    copies = [
        pltpu.make_async_copy(src, dst, sems.at[i]) for i, (src, dst) in enumerate(pairs)
    ]
    for copy in copies:
        copy.start()
    return copies


def load_kernel(
    leaf, rhs_hbm, inv_hbm, two_hbm, three_hbm, one_hbm, cap_hbm,
    gram_send, gram_keep, field, two, three, one, cap, rhs, inv, gram, sems,
):
    n = rhs.shape[0]
    leaves = n // leaf
    pairs = []
    for i in range(leaves):
        rows = pl.ds(i * leaf, leaf)
        pairs.append((rhs_hbm.at[rows], rhs.at[rows]))
        pairs.append((inv_hbm.at[rows], inv.at[rows]))
    pairs += [(two_hbm, two), (three_hbm, three), (one_hbm, one), (cap_hbm, cap)]
    copies = fetch(pairs, sems)
    for i in range(leaves):
        rows = pl.ds(i * leaf, leaf)
        copies[2 * i].wait()
        flipped = jnp.transpose(rhs[rows, :])
        copies[2 * i + 1].wait()
        field[:, i * leaf : (i + 1) * leaf] = nt(flipped, inv[rows, :])
    copies[2 * leaves].wait()
    copies[2 * leaves + 1].wait()
    gram[...] = tn(two[...], three[...])
    half = gram_keep.shape[0]
    me = lax.axis_index("sub")
    gram_keep[...] = gram[pl.ds(pl.multiple_of(me * half, half), half), :]
    gram_send[...] = gram[pl.ds(pl.multiple_of((1 - me) * half, half), half), :]
    copies[2 * leaves + 2].wait()
    copies[2 * leaves + 3].wait()


def local_kernel(leaf, field, one, cap, two, three, field_out, send, keep, proj):
    m, n = field.shape
    leaves = n // leaf
    rank = one.shape[1]
    width = m // 4
    fields = [field[:, i * leaf : (i + 1) * leaf] for i in range(leaves)]
    bases = [one[pl.ds(i * leaf, leaf), :] for i in range(leaves)]
    projected = [nn(f.astype(BF16), b) for f, b in zip(fields, bases)]
    for i in range(0, leaves, 2):
        stacked = jnp.concatenate(projected[i : i + 2], axis=1)
        coef = exact_nt(stacked, cap[...]).astype(BF16)
        for j in range(2):
            fields[i + j] = fields[i + j] - nt(coef[:, j * rank : (j + 1) * rank], bases[i + j])
    total = jnp.concatenate(fields, axis=1)
    field_out[...] = total
    high, low = split(total, 2)
    proj[0] = nn(high, two[...])
    proj[1] = nn(high, three[...]) + nn(low, three[...])
    me = lax.axis_index("sub")
    for side in range(2):
        for level in range(2):
            for ref, core in ((keep, me), (send, 1 - me)):
                start = pl.multiple_of(side * 2 * width + core * width, width)
                ref[side, level] = proj[level, pl.ds(start, width), :]


def middle_kernel(
    bit, mine, other, cap, gram_own, gram_far, gram_swap, total_out, coef_own, coef_other, gram
):
    rank = mine.shape[2]
    half = rank // 2
    me = lax.axis_index("sub")
    here = pl.ds(pl.multiple_of(me * half, half), half)
    there = pl.ds(pl.multiple_of((1 - me) * half, half), half)
    for i, part in enumerate((gram_own, gram_far)):
        gram[i, here, :] = part[...]
        gram[i, there, :] = gram_swap[i]
    side = (lax.axis_index("row") >> bit) & 1
    own, far = mine[0], other[0]
    is_first = side == 0
    stacked = jnp.concatenate(
        [jnp.where(is_first, own, far), jnp.where(is_first, far, own)], axis=1
    )
    coef = exact_nt(stacked, cap[...]).astype(BF16)
    left, right = coef[:, :rank].astype(F32), coef[:, rank:].astype(F32)
    c_own = jnp.where(is_first, left, right)
    c_far = jnp.where(is_first, right, left)
    coef_own[...] = c_own
    coef_other[...] = c_far
    total = mine[1] + other[1]
    for i, c in enumerate((c_own, c_far)):
        c = c.astype(BF16)
        for part in split(gram[i], 3):
            total = total - nn(c, part)
    total_out[...] = total


def last_coef_kernel(bit, mine, other, cap, out):
    rank = mine.shape[1]
    side = (lax.axis_index("row") >> bit) & 1
    is_first = side == 0
    own, far = mine[...], other[...]
    stacked = jnp.concatenate(
        [jnp.where(is_first, own, far), jnp.where(is_first, far, own)], axis=1
    )
    rows = cap[pl.ds(pl.multiple_of(side * rank, rank), rank), :]
    out[...] = exact_nt(stacked, rows).astype(BF16).astype(F32)


def gather_coef(bit, own, across, cores, scratch):
    width = own.shape[0]
    me = lax.axis_index("sub")
    side = (lax.axis_index("row") >> bit) & 1

    def put(s, c, value):
        start = pl.multiple_of((s * 2 + c) * width, width)
        scratch[pl.ds(start, width), :] = value.astype(BF16)

    put(side, me, own[...])
    put(1 - side, me, across[...])
    put(side, 1 - me, cores[0])
    put(1 - side, 1 - me, cores[1])


def base_kernel(bit, field, own, across, cores, two, out, scratch):
    gather_coef(bit, own, across, cores, scratch)
    out[...] = jnp.transpose(field[...]) - nt(two[...], scratch[...])


def final_kernel(bit, base, own, across, cores, three, out, scratch):
    gather_coef(bit, own, across, cores, scratch)
    out[...] = (base[...] - nt(three[...], scratch[...])).astype(BF16)


def share(own, across):
    return partner(jnp.stack([own, across]), "sub", 0)


def per_device(
    right_sides,
    leaf_inverse,
    basis_one,
    basis_two,
    basis_three,
    capacity_one,
    capacity_two,
    capacity_three,
):
    n, m = right_sides.shape
    leaf = leaf_inverse.shape[1]
    rank = basis_one.shape[1]
    leaves = n // leaf
    width = m // 4
    row_count = lax.axis_size("row")
    row_index = lax.axis_index("row")
    bit_two = (row_count // 8).bit_length() - 1
    bit_three = (row_count // 2).bit_length() - 1
    side = (row_index >> bit_two) & 1

    gram_send, gram_half, field, two, three, one, cap = pl.pallas_call(
        functools.partial(load_kernel, leaf),
        out_shape=[
            jax.ShapeDtypeStruct((rank // 2, rank), F32),
            jax.ShapeDtypeStruct((rank // 2, rank), F32),
            jax.ShapeDtypeStruct((m, n), F32),
            jax.ShapeDtypeStruct((n, rank), BF16),
            jax.ShapeDtypeStruct((n, rank), BF16),
            jax.ShapeDtypeStruct((n, rank), BF16),
            jax.ShapeDtypeStruct(capacity_one.shape, BF16),
        ],
        in_specs=[pl.BlockSpec(memory_space=pltpu.HBM)] * 6,
        out_specs=[VM] * 7,
        scratch_shapes=[
            pltpu.VMEM((n, m), BF16),
            pltpu.VMEM((n, leaf), BF16),
            pltpu.VMEM((rank, rank), F32),
            pltpu.SemaphoreType.DMA((2 * leaves + 4,)),
        ],
        compiler_params=params(12288),
        name="load",
    )(*(
        pltpu.with_memory_space_constraint(x, pltpu.HBM)
        for x in (right_sides, leaf_inverse, basis_two, basis_three, basis_one, capacity_one)
    ))
    gram_half = gram_half + partner(gram_send, "sub", 0)

    field, send, keep = pl.pallas_call(
        functools.partial(local_kernel, leaf),
        out_shape=[
            jax.ShapeDtypeStruct((m, n), F32),
            jax.ShapeDtypeStruct((2, 2, width, rank), F32),
            jax.ShapeDtypeStruct((2, 2, width, rank), F32),
        ],
        in_specs=[VM] * 5,
        out_specs=[VM, VM, VM],
        scratch_shapes=[pltpu.VMEM((2, m, rank), F32)],
        compiler_params=params(12288),
        name="local",
    )(field, one, cap, two, three)

    both = keep + partner(send, "sub", 0)
    for bit in range(bit_two):
        both = both + partner(both, "row", bit)
        gram_half = gram_half + partner(gram_half, "row", bit)
    gram_far = partner(gram_half, "row", bit_two)
    gram_swap = share(gram_half, gram_far)

    mine = lax.dynamic_index_in_dim(both, side, 0, keepdims=False)
    theirs = lax.dynamic_index_in_dim(both, 1 - side, 0, keepdims=False)
    other = partner(theirs, "row", bit_two)
    piece = jax.ShapeDtypeStruct((width, rank), F32)
    total, two_own, two_far = pl.pallas_call(
        functools.partial(middle_kernel, bit_two),
        out_shape=[piece, piece, piece],
        in_specs=[VM] * 6,
        out_specs=[VM] * 3,
        scratch_shapes=[pltpu.VMEM((2, rank, rank), F32)],
        compiler_params=params(4096),
        name="middle",
    )(mine, other, capacity_two, gram_half, gram_far, gram_swap)

    for bit in range(bit_two + 1, bit_three):
        total = total + partner(total, "row", bit)
    sibling = partner(total, "row", bit_three)

    two_across = partner(two_far, "row", bit_two)
    two_cores = share(two_own, two_across)
    base = pl.pallas_call(
        functools.partial(base_kernel, bit_two),
        out_shape=jax.ShapeDtypeStruct((n, m), F32),
        in_specs=[VM] * 5,
        out_specs=VM,
        scratch_shapes=[pltpu.VMEM((m, rank), BF16)],
        compiler_params=params(8192),
        name="base",
    )(field, two_own, two_across, two_cores, two)

    three_own = pl.pallas_call(
        functools.partial(last_coef_kernel, bit_three),
        out_shape=piece,
        in_specs=[VM] * 3,
        out_specs=VM,
        compiler_params=params(2048),
        name="last_coef",
    )(total, sibling, capacity_three)
    three_across = partner(three_own, "row", bit_two)
    three_cores = share(three_own, three_across)
    return pl.pallas_call(
        functools.partial(final_kernel, bit_two),
        out_shape=jax.ShapeDtypeStruct((n, m), BF16),
        in_specs=[VM] * 5,
        out_specs=VM,
        scratch_shapes=[pltpu.VMEM((m, rank), BF16)],
        compiler_params=params(8192),
        name="final",
    )(base, three_own, three_across, three_cores, three)


def solution(mesh):
    rows = P(("grp", "row", "sub"), None)

    return jax.shard_map(
        per_device,
        mesh=mesh,
        in_specs=(rows,) * 5 + (P("grp", None),) * 3,
        out_specs=rows,
        check_vma=False,
    )
```

```python
import functools

import jax
import jax.numpy as jnp
from jax import lax
from jax.experimental import pallas as pl
from jax.experimental.pallas import tpu as pltpu
from jax.sharding import PartitionSpec as P


F32, BF16 = jnp.float32, jnp.bfloat16
VM = pl.BlockSpec(memory_space=pltpu.VMEM)
HB = pl.BlockSpec(memory_space=pl.ANY)


def nn(a, b):
    return lax.dot_general(a, b, (((1,), (0,)), ((), ())), preferred_element_type=F32)


def nt(a, b):
    return lax.dot_general(a, b, (((1,), (1,)), ((), ())), preferred_element_type=F32)


def tn(a, b):
    return lax.dot_general(a, b, (((0,), (0,)), ((), ())), preferred_element_type=F32)


def split(x, terms):
    parts = []
    for _ in range(terms - 1):
        part = x.astype(BF16)
        parts.append(part)
        x = x - part.astype(F32)
    parts.append(x.astype(BF16))
    return parts


def exact_nt(x, capacity):
    rows = x.shape[0]
    out = nt(jnp.concatenate(split(x, 3), axis=0), capacity)
    return out[:rows] + (out[rows : 2 * rows] + out[2 * rows :])


def partner(array, axis, bit):
    return lax.ppermute(array, axis, [(i, i ^ 1 << bit) for i in range(lax.axis_size(axis))])


def params(kib):
    return pltpu.CompilerParams(vmem_limit_bytes=kib * 1024)


def fetch(pairs, sems):
    copies = [
        pltpu.make_async_copy(src, dst, sems.at[i]) for i, (src, dst) in enumerate(pairs)
    ]
    for copy in copies:
        copy.start()
    return copies


def load_kernel(
    leaf, rhs_hbm, inv_hbm, two_hbm, three_hbm, one_hbm, cap_hbm,
    gram_send, gram_keep, field, coef, two, three, one, cap, rhs, inv, gram, sems,
):
    n = rhs.shape[0]
    rank = one.shape[1]
    leaves = n // leaf
    pairs = []
    for i in range(leaves):
        rows = pl.ds(i * leaf, leaf)
        pairs.append((rhs_hbm.at[rows], rhs.at[rows]))
        pairs.append((inv_hbm.at[rows], inv.at[rows]))
    pairs += [(two_hbm, two), (three_hbm, three), (one_hbm, one), (cap_hbm, cap)]
    copies = fetch(pairs, sems)
    fields = []
    for i in range(leaves):
        rows = pl.ds(i * leaf, leaf)
        copies[2 * i].wait()
        flipped = jnp.transpose(rhs[rows, :])
        copies[2 * i + 1].wait()
        fields.append(nt(flipped, inv[rows, :]))
        field[:, i * leaf : (i + 1) * leaf] = fields[i]
    copies[2 * leaves].wait()
    copies[2 * leaves + 1].wait()
    gram[...] = tn(two[...], three[...])
    half = gram_keep.shape[0]
    me = lax.axis_index("sub")
    gram_keep[...] = gram[pl.ds(pl.multiple_of(me * half, half), half), :]
    gram_send[...] = gram[pl.ds(pl.multiple_of((1 - me) * half, half), half), :]
    copies[2 * leaves + 2].wait()
    projected = [
        nn(f.astype(BF16), one[pl.ds(i * leaf, leaf), :]) for i, f in enumerate(fields)
    ]
    copies[2 * leaves + 3].wait()
    for i in range(0, leaves, 2):
        stacked = jnp.concatenate(projected[i : i + 2], axis=1)
        coef[:, i * rank : (i + 2) * rank] = exact_nt(stacked, cap[...]).astype(BF16)


def local_kernel(leaf, field, coef, one, two, three, field_out, send, keep, proj):
    m, n = field.shape
    leaves = n // leaf
    rank = one.shape[1]
    width = m // 4
    total = jnp.concatenate(
        [
            field[:, i * leaf : (i + 1) * leaf]
            - nt(coef[:, i * rank : (i + 1) * rank], one[pl.ds(i * leaf, leaf), :])
            for i in range(leaves)
        ],
        axis=1,
    )
    field_out[...] = total
    high, low = split(total, 2)
    proj[0] = nn(high, two[...])
    both = nn(jnp.concatenate([high, low], axis=0), three[...])
    proj[1] = both[:m] + both[m:]
    me = lax.axis_index("sub")
    for side in range(2):
        for level in range(2):
            for ref, core in ((keep, me), (send, 1 - me)):
                start = pl.multiple_of(side * 2 * width + core * width, width)
                ref[side, level] = proj[level, pl.ds(start, width), :]


def middle_kernel(
    bit, mine, other, cap, gram_own, gram_far, gram_swap, total_out, coef_own, coef_other, gram
):
    rank = mine.shape[2]
    half = rank // 2
    me = lax.axis_index("sub")
    here = pl.ds(pl.multiple_of(me * half, half), half)
    there = pl.ds(pl.multiple_of((1 - me) * half, half), half)
    for i, part in enumerate((gram_own, gram_far)):
        gram[i, here, :] = part[...]
        gram[i, there, :] = gram_swap[i]
    side = (lax.axis_index("row") >> bit) & 1
    own, far = mine[0], other[0]
    is_first = side == 0
    stacked = jnp.concatenate(
        [jnp.where(is_first, own, far), jnp.where(is_first, far, own)], axis=1
    )
    coef = exact_nt(stacked, cap[...]).astype(BF16)
    left, right = coef[:, :rank].astype(F32), coef[:, rank:].astype(F32)
    c_own = jnp.where(is_first, left, right)
    c_far = jnp.where(is_first, right, left)
    coef_own[...] = c_own
    coef_other[...] = c_far
    total = mine[1] + other[1]
    for i, c in enumerate((c_own, c_far)):
        c = c.astype(BF16)
        for part in split(gram[i], 3):
            total = total - nn(c, part)
    total_out[...] = total


def last_coef_kernel(bit, mine, other, cap, out):
    rank = mine.shape[1]
    side = (lax.axis_index("row") >> bit) & 1
    is_first = side == 0
    own, far = mine[...], other[...]
    stacked = jnp.concatenate(
        [jnp.where(is_first, own, far), jnp.where(is_first, far, own)], axis=1
    )
    rows = cap[pl.ds(pl.multiple_of(side * rank, rank), rank), :]
    out[...] = exact_nt(stacked, rows).astype(BF16).astype(F32)


def gather_coef(bit, own, across, cores, scratch):
    width = own.shape[0]
    me = lax.axis_index("sub")
    side = (lax.axis_index("row") >> bit) & 1

    def put(s, c, value):
        start = pl.multiple_of((s * 2 + c) * width, width)
        scratch[pl.ds(start, width), :] = value.astype(BF16)

    put(side, me, own[...])
    put(1 - side, me, across[...])
    put(side, 1 - me, cores[0])
    put(1 - side, 1 - me, cores[1])


def base_kernel(bit, field, own, across, cores, two, out, scratch):
    gather_coef(bit, own, across, cores, scratch)
    out[...] = jnp.transpose(field[...]) - nt(two[...], scratch[...])


def final_kernel(bit, base, own, across, cores, three, out_hbm, scratch, out, sems):
    gather_coef(bit, own, across, cores, scratch)
    chunks = sems.shape[0]
    size = out.shape[0] // chunks
    copies = []
    for i in range(chunks):
        rows = pl.ds(i * size, size)
        out[rows, :] = (base[rows, :] - nt(three[rows, :], scratch[...])).astype(BF16)
        copies.append(pltpu.make_async_copy(out.at[rows], out_hbm.at[rows], sems.at[i]))
        copies[-1].start()
    for copy in copies:
        copy.wait()


def share(own, across):
    return partner(jnp.stack([own, across]), "sub", 0)


def per_device(
    right_sides,
    leaf_inverse,
    basis_one,
    basis_two,
    basis_three,
    capacity_one,
    capacity_two,
    capacity_three,
):
    n, m = right_sides.shape
    leaf = leaf_inverse.shape[1]
    rank = basis_one.shape[1]
    leaves = n // leaf
    width = m // 4
    row_count = lax.axis_size("row")
    row_index = lax.axis_index("row")
    bit_two = (row_count // 8).bit_length() - 1
    bit_three = (row_count // 2).bit_length() - 1
    side = (row_index >> bit_two) & 1

    gram_send, gram_half, field, coef, two, three, one = pl.pallas_call(
        functools.partial(load_kernel, leaf),
        out_shape=[
            jax.ShapeDtypeStruct((rank // 2, rank), F32),
            jax.ShapeDtypeStruct((rank // 2, rank), F32),
            jax.ShapeDtypeStruct((m, n), F32),
            jax.ShapeDtypeStruct((m, leaves * rank), BF16),
            jax.ShapeDtypeStruct((n, rank), BF16),
            jax.ShapeDtypeStruct((n, rank), BF16),
            jax.ShapeDtypeStruct((n, rank), BF16),
        ],
        in_specs=[pl.BlockSpec(memory_space=pltpu.HBM)] * 6,
        out_specs=[VM] * 7,
        scratch_shapes=[
            pltpu.VMEM(capacity_one.shape, BF16),
            pltpu.VMEM((n, m), BF16),
            pltpu.VMEM((n, leaf), BF16),
            pltpu.VMEM((rank, rank), F32),
            pltpu.SemaphoreType.DMA((2 * leaves + 4,)),
        ],
        compiler_params=params(12288),
        name="load",
    )(*(
        pltpu.with_memory_space_constraint(x, pltpu.HBM)
        for x in (right_sides, leaf_inverse, basis_two, basis_three, basis_one, capacity_one)
    ))
    gram_half = gram_half + partner(gram_send, "sub", 0)

    field, send, keep = pl.pallas_call(
        functools.partial(local_kernel, leaf),
        out_shape=[
            jax.ShapeDtypeStruct((m, n), F32),
            jax.ShapeDtypeStruct((2, 2, width, rank), F32),
            jax.ShapeDtypeStruct((2, 2, width, rank), F32),
        ],
        in_specs=[VM] * 5,
        out_specs=[VM] * 3,
        scratch_shapes=[pltpu.VMEM((2, m, rank), F32)],
        compiler_params=params(8192),
        name="local",
    )(field, coef, one, two, three)

    both = keep + partner(send, "sub", 0)
    for bit in range(bit_two):
        both = both + partner(both, "row", bit)
        gram_half = gram_half + partner(gram_half, "row", bit)
    gram_far = partner(gram_half, "row", bit_two)
    gram_swap = share(gram_half, gram_far)

    mine = lax.dynamic_index_in_dim(both, side, 0, keepdims=False)
    theirs = lax.dynamic_index_in_dim(both, 1 - side, 0, keepdims=False)
    other = partner(theirs, "row", bit_two)
    piece = jax.ShapeDtypeStruct((width, rank), F32)
    total, two_own, two_far = pl.pallas_call(
        functools.partial(middle_kernel, bit_two),
        out_shape=[piece, piece, piece],
        in_specs=[VM] * 6,
        out_specs=[VM] * 3,
        scratch_shapes=[pltpu.VMEM((2, rank, rank), F32)],
        compiler_params=params(4096),
        name="middle",
    )(mine, other, capacity_two, gram_half, gram_far, gram_swap)

    for bit in range(bit_two + 1, bit_three):
        total = total + partner(total, "row", bit)
    sibling = partner(total, "row", bit_three)

    two_across = partner(two_far, "row", bit_two)
    two_cores = share(two_own, two_across)
    base = pl.pallas_call(
        functools.partial(base_kernel, bit_two),
        out_shape=jax.ShapeDtypeStruct((n, m), F32),
        in_specs=[VM] * 5,
        out_specs=VM,
        scratch_shapes=[pltpu.VMEM((m, rank), BF16)],
        compiler_params=params(8192),
        name="base",
    )(field, two_own, two_across, two_cores, two)

    three_own = pl.pallas_call(
        functools.partial(last_coef_kernel, bit_three),
        out_shape=piece,
        in_specs=[VM] * 3,
        out_specs=VM,
        compiler_params=params(2048),
        name="last_coef",
    )(total, sibling, capacity_three)
    three_across = partner(three_own, "row", bit_two)
    three_cores = share(three_own, three_across)
    return pl.pallas_call(
        functools.partial(final_kernel, bit_two),
        out_shape=jax.ShapeDtypeStruct((n, m), BF16),
        in_specs=[VM] * 5,
        out_specs=HB,
        scratch_shapes=[
            pltpu.VMEM((m, rank), BF16),
            pltpu.VMEM((n, m), BF16),
            pltpu.SemaphoreType.DMA((4,)),
        ],
        compiler_params=params(8192),
        name="final",
    )(base, three_own, three_across, three_cores, three)


def solution(mesh):
    rows = P(("grp", "row", "sub"), None)

    return jax.shard_map(
        per_device,
        mesh=mesh,
        in_specs=(rows,) * 5 + (P("grp", None),) * 3,
        out_specs=rows,
        check_vma=False,
    )
```

```python
import functools

import jax
import jax.numpy as jnp
from jax import lax
from jax.experimental import pallas as pl
from jax.experimental.pallas import tpu as pltpu
from jax.sharding import PartitionSpec as P


F32, BF16 = jnp.float32, jnp.bfloat16
VM = pl.BlockSpec(memory_space=pltpu.VMEM)
HB = pl.BlockSpec(memory_space=pl.ANY)


def nn(a, b):
    return lax.dot_general(a, b, (((1,), (0,)), ((), ())), preferred_element_type=F32)


def nt(a, b):
    return lax.dot_general(a, b, (((1,), (1,)), ((), ())), preferred_element_type=F32)


def tn(a, b):
    return lax.dot_general(a, b, (((0,), (0,)), ((), ())), preferred_element_type=F32)


def split(x, terms):
    parts = []
    for _ in range(terms - 1):
        part = x.astype(BF16)
        parts.append(part)
        x = x - part.astype(F32)
    parts.append(x.astype(BF16))
    return parts


def exact_nt(x, capacity):
    rows = x.shape[0]
    out = nt(jnp.concatenate(split(x, 2), axis=0), capacity)
    return out[:rows] + out[rows:]


def partner(array, axis, bit):
    return lax.ppermute(array, axis, [(i, i ^ 1 << bit) for i in range(lax.axis_size(axis))])


def params(kib):
    return pltpu.CompilerParams(vmem_limit_bytes=kib * 1024)


def fetch(pairs, sems):
    copies = [
        pltpu.make_async_copy(src, dst, sems.at[i]) for i, (src, dst) in enumerate(pairs)
    ]
    for copy in copies:
        copy.start()
    return copies


def load_kernel(
    leaf, rhs_hbm, inv_hbm, two_hbm, three_hbm, one_hbm, cap_hbm,
    gram_send, gram_keep, field, coef, two, three, one, cap, rhs, inv, gram, sems,
):
    n = rhs.shape[0]
    rank = one.shape[1]
    leaves = n // leaf
    pairs = []
    for i in range(leaves):
        rows = pl.ds(i * leaf, leaf)
        pairs.append((rhs_hbm.at[rows], rhs.at[rows]))
        pairs.append((inv_hbm.at[rows], inv.at[rows]))
    pairs += [(one_hbm, one), (two_hbm, two), (three_hbm, three), (cap_hbm, cap)]
    copies = fetch(pairs, sems)

    def solve(i):
        rows = pl.ds(i * leaf, leaf)
        field[:, i * leaf : (i + 1) * leaf] = nt(jnp.transpose(rhs[rows, :]), inv[rows, :])

    def onto_one(i):
        part = field[:, i * leaf : (i + 1) * leaf].astype(BF16)
        return nn(part, one[pl.ds(i * leaf, leaf), :])

    for copy in copies[:2]:
        copy.wait()
    solve(0)
    for copy in copies[2 : 2 * leaves + 1]:
        copy.wait()
    for i in range(1, leaves):
        solve(i)
    projected = [onto_one(i) for i in range(leaves)]
    for copy in copies[2 * leaves + 1 :]:
        copy.wait()
    gram[...] = tn(two[...], three[...])
    for i in range(0, leaves, 2):
        stacked = jnp.concatenate(projected[i : i + 2], axis=1)
        coef[:, i * rank : (i + 2) * rank] = exact_nt(stacked, cap[...]).astype(BF16)
    half = gram_keep.shape[0]
    me = lax.axis_index("sub")
    gram_keep[...] = gram[pl.ds(pl.multiple_of(me * half, half), half), :]
    gram_send[...] = gram[pl.ds(pl.multiple_of((1 - me) * half, half), half), :]


def local_kernel(leaf, field, coef, one, two, three, field_out, send, keep, proj):
    m, n = field.shape
    leaves = n // leaf
    rank = one.shape[1]
    width = m // 4
    total = jnp.concatenate(
        [
            field[:, i * leaf : (i + 1) * leaf]
            - nt(coef[:, i * rank : (i + 1) * rank], one[pl.ds(i * leaf, leaf), :])
            for i in range(leaves)
        ],
        axis=1,
    )
    field_out[...] = total
    high, low = split(total, 2)
    proj[0] = nn(high, two[...])
    both = nn(jnp.concatenate([high, low], axis=0), three[...])
    proj[1] = both[:m] + both[m:]
    me = lax.axis_index("sub")
    for side in range(2):
        for level in range(2):
            for ref, core in ((keep, me), (send, 1 - me)):
                start = pl.multiple_of(side * 2 * width + core * width, width)
                ref[side, level] = proj[level, pl.ds(start, width), :]


def middle_kernel(
    bit, mine, other, cap, gram_own, gram_far, gram_swap, total_out, coef_own, coef_other, gram
):
    rank = mine.shape[2]
    half = rank // 2
    me = lax.axis_index("sub")
    here = pl.ds(pl.multiple_of(me * half, half), half)
    there = pl.ds(pl.multiple_of((1 - me) * half, half), half)
    for i, part in enumerate((gram_own, gram_far)):
        gram[i, here, :] = part[...]
        gram[i, there, :] = gram_swap[i]
    side = (lax.axis_index("row") >> bit) & 1
    own, far = mine[0], other[0]
    is_first = side == 0
    stacked = jnp.concatenate(
        [jnp.where(is_first, own, far), jnp.where(is_first, far, own)], axis=1
    )
    coef = exact_nt(stacked, cap[...]).astype(BF16)
    left, right = coef[:, :rank].astype(F32), coef[:, rank:].astype(F32)
    c_own = jnp.where(is_first, left, right)
    c_far = jnp.where(is_first, right, left)
    coef_own[...] = c_own
    coef_other[...] = c_far
    total = mine[1] + other[1]
    for i, c in enumerate((c_own, c_far)):
        c = c.astype(BF16)
        for part in split(gram[i], 2):
            total = total - nn(c, part)
    total_out[...] = total


def last_coef_kernel(bit, mine, other, cap, out):
    rank = mine.shape[1]
    side = (lax.axis_index("row") >> bit) & 1
    is_first = side == 0
    own, far = mine[...], other[...]
    stacked = jnp.concatenate(
        [jnp.where(is_first, own, far), jnp.where(is_first, far, own)], axis=1
    )
    rows = cap[pl.ds(pl.multiple_of(side * rank, rank), rank), :]
    out[...] = exact_nt(stacked, rows).astype(BF16).astype(F32)


def gather_coef(bit, own, across, cores, scratch):
    width = own.shape[0]
    me = lax.axis_index("sub")
    side = (lax.axis_index("row") >> bit) & 1

    def put(s, c, value):
        start = pl.multiple_of((s * 2 + c) * width, width)
        scratch[pl.ds(start, width), :] = value.astype(BF16)

    put(side, me, own[...])
    put(1 - side, me, across[...])
    put(side, 1 - me, cores[0])
    put(1 - side, 1 - me, cores[1])


def base_kernel(bit, field, own, across, cores, two, out, scratch):
    gather_coef(bit, own, across, cores, scratch)
    out[...] = jnp.transpose(field[...]) - nt(two[...], scratch[...])


def final_kernel(bit, base, own, across, cores, three, out_hbm, scratch, out, sems):
    gather_coef(bit, own, across, cores, scratch)
    chunks = sems.shape[0]
    size = out.shape[0] // chunks
    copies = []
    for i in range(chunks):
        rows = pl.ds(i * size, size)
        out[rows, :] = (base[rows, :] - nt(three[rows, :], scratch[...])).astype(BF16)
        copies.append(pltpu.make_async_copy(out.at[rows], out_hbm.at[rows], sems.at[i]))
        copies[-1].start()
    for copy in copies:
        copy.wait()


def share(own, across):
    return partner(jnp.stack([own, across]), "sub", 0)


def per_device(
    right_sides,
    leaf_inverse,
    basis_one,
    basis_two,
    basis_three,
    capacity_one,
    capacity_two,
    capacity_three,
):
    n, m = right_sides.shape
    leaf = leaf_inverse.shape[1]
    rank = basis_one.shape[1]
    leaves = n // leaf
    width = m // 4
    row_count = lax.axis_size("row")
    row_index = lax.axis_index("row")
    bit_two = (row_count // 8).bit_length() - 1
    bit_three = (row_count // 2).bit_length() - 1
    side = (row_index >> bit_two) & 1

    gram_send, gram_half, field, coef, two, three, one = pl.pallas_call(
        functools.partial(load_kernel, leaf),
        out_shape=[
            jax.ShapeDtypeStruct((rank // 2, rank), F32),
            jax.ShapeDtypeStruct((rank // 2, rank), F32),
            jax.ShapeDtypeStruct((m, n), F32),
            jax.ShapeDtypeStruct((m, leaves * rank), BF16),
            jax.ShapeDtypeStruct((n, rank), BF16),
            jax.ShapeDtypeStruct((n, rank), BF16),
            jax.ShapeDtypeStruct((n, rank), BF16),
        ],
        in_specs=[pl.BlockSpec(memory_space=pltpu.HBM)] * 6,
        out_specs=[VM] * 7,
        scratch_shapes=[
            pltpu.VMEM(capacity_one.shape, BF16),
            pltpu.VMEM((n, m), BF16),
            pltpu.VMEM((n, leaf), BF16),
            pltpu.VMEM((rank, rank), F32),
            pltpu.SemaphoreType.DMA((2 * leaves + 4,)),
        ],
        compiler_params=params(12288),
        name="load",
    )(*(
        pltpu.with_memory_space_constraint(x, pltpu.HBM)
        for x in (right_sides, leaf_inverse, basis_two, basis_three, basis_one, capacity_one)
    ))
    gram_half = gram_half + partner(gram_send, "sub", 0)

    field, send, keep = pl.pallas_call(
        functools.partial(local_kernel, leaf),
        out_shape=[
            jax.ShapeDtypeStruct((m, n), F32),
            jax.ShapeDtypeStruct((2, 2, width, rank), F32),
            jax.ShapeDtypeStruct((2, 2, width, rank), F32),
        ],
        in_specs=[VM] * 5,
        out_specs=[VM] * 3,
        scratch_shapes=[pltpu.VMEM((2, m, rank), F32)],
        compiler_params=params(8192),
        name="local",
    )(field, coef, one, two, three)

    both = keep + partner(send, "sub", 0)
    for bit in range(bit_two):
        both = both + partner(both, "row", bit)
        gram_half = gram_half + partner(gram_half, "row", bit)
    gram_far = partner(gram_half, "row", bit_two)
    gram_swap = share(gram_half, gram_far)

    mine = lax.dynamic_index_in_dim(both, side, 0, keepdims=False)
    theirs = lax.dynamic_index_in_dim(both, 1 - side, 0, keepdims=False)
    other = partner(theirs, "row", bit_two)
    piece = jax.ShapeDtypeStruct((width, rank), F32)
    total, two_own, two_far = pl.pallas_call(
        functools.partial(middle_kernel, bit_two),
        out_shape=[piece, piece, piece],
        in_specs=[VM] * 6,
        out_specs=[VM] * 3,
        scratch_shapes=[pltpu.VMEM((2, rank, rank), F32)],
        compiler_params=params(4096),
        name="middle",
    )(mine, other, capacity_two, gram_half, gram_far, gram_swap)

    for bit in range(bit_two + 1, bit_three):
        total = total + partner(total, "row", bit)
    sibling = partner(total, "row", bit_three)

    two_across = partner(two_far, "row", bit_two)
    two_cores = share(two_own, two_across)
    base = pl.pallas_call(
        functools.partial(base_kernel, bit_two),
        out_shape=jax.ShapeDtypeStruct((n, m), F32),
        in_specs=[VM] * 5,
        out_specs=VM,
        scratch_shapes=[pltpu.VMEM((m, rank), BF16)],
        compiler_params=params(8192),
        name="base",
    )(field, two_own, two_across, two_cores, two)

    three_own = pl.pallas_call(
        functools.partial(last_coef_kernel, bit_three),
        out_shape=piece,
        in_specs=[VM] * 3,
        out_specs=VM,
        compiler_params=params(2048),
        name="last_coef",
    )(total, sibling, capacity_three)
    three_across = partner(three_own, "row", bit_two)
    three_cores = share(three_own, three_across)
    return pl.pallas_call(
        functools.partial(final_kernel, bit_two),
        out_shape=jax.ShapeDtypeStruct((n, m), BF16),
        in_specs=[VM] * 5,
        out_specs=HB,
        scratch_shapes=[
            pltpu.VMEM((m, rank), BF16),
            pltpu.VMEM((n, m), BF16),
            pltpu.SemaphoreType.DMA((4,)),
        ],
        compiler_params=params(8192),
        name="final",
    )(base, three_own, three_across, three_cores, three)


def solution(mesh):
    rows = P(("grp", "row", "sub"), None)

    return jax.shard_map(
        per_device,
        mesh=mesh,
        in_specs=(rows,) * 5 + (P("grp", None),) * 3,
        out_specs=rows,
        check_vma=False,
    )
```

```python
import functools

import jax
import jax.numpy as jnp
from jax import lax
from jax.experimental import pallas as pl
from jax.experimental.pallas import tpu as pltpu
from jax.sharding import PartitionSpec as P


F32, BF16 = jnp.float32, jnp.bfloat16
VM = pl.BlockSpec(memory_space=pltpu.VMEM)
HB = pl.BlockSpec(memory_space=pl.ANY)


def nn(a, b):
    return lax.dot_general(a, b, (((1,), (0,)), ((), ())), preferred_element_type=F32)


def nt(a, b):
    return lax.dot_general(a, b, (((1,), (1,)), ((), ())), preferred_element_type=F32)


def tn(a, b):
    return lax.dot_general(a, b, (((0,), (0,)), ((), ())), preferred_element_type=F32)


def split(x, terms):
    parts = []
    for _ in range(terms - 1):
        part = x.astype(BF16)
        parts.append(part)
        x = x - part.astype(F32)
    parts.append(x.astype(BF16))
    return parts


def exact_nt(x, capacity):
    rows = x.shape[0]
    out = nt(jnp.concatenate(split(x, 2), axis=0), capacity)
    return out[:rows] + out[rows:]


def partner(array, axis, bit):
    return lax.ppermute(array, axis, [(i, i ^ 1 << bit) for i in range(lax.axis_size(axis))])


def across_chips(array, bit):
    cores = lax.axis_size("sub")
    mask = cores << bit | 1
    count = cores * lax.axis_size("row")
    return lax.ppermute(array, ("row", "sub"), [(i, i ^ mask) for i in range(count)])


def place(bit):
    side = (lax.axis_index("row") >> bit) & 1
    return side, lax.axis_index("sub") ^ side


def params(kib):
    return pltpu.CompilerParams(vmem_limit_bytes=kib * 1024)


def fetch(pairs, sems):
    copies = [
        pltpu.make_async_copy(src, dst, sems.at[i]) for i, (src, dst) in enumerate(pairs)
    ]
    for copy in copies:
        copy.start()
    return copies


def load_kernel(
    leaf, bit, rhs_hbm, inv_hbm, two_hbm, three_hbm, one_hbm, cap_hbm,
    gram_send, gram_keep, field, coef, two, three, one, cap, rhs, inv, gram, sems,
):
    n = rhs.shape[0]
    rank = one.shape[1]
    leaves = n // leaf
    pairs = []
    for i in range(leaves):
        rows = pl.ds(i * leaf, leaf)
        pairs.append((rhs_hbm.at[rows], rhs.at[rows]))
        pairs.append((inv_hbm.at[rows], inv.at[rows]))
    pairs += [(one_hbm, one), (two_hbm, two), (three_hbm, three), (cap_hbm, cap)]
    copies = fetch(pairs, sems)

    def solve(i):
        rows = pl.ds(i * leaf, leaf)
        field[:, i * leaf : (i + 1) * leaf] = nt(jnp.transpose(rhs[rows, :]), inv[rows, :])

    def onto_one(i):
        part = field[:, i * leaf : (i + 1) * leaf].astype(BF16)
        return nn(part, one[pl.ds(i * leaf, leaf), :])

    for copy in copies[:2]:
        copy.wait()
    solve(0)
    for copy in copies[2 : 2 * leaves + 1]:
        copy.wait()
    for i in range(1, leaves):
        solve(i)
    projected = [onto_one(i) for i in range(leaves)]
    for copy in copies[2 * leaves + 1 :]:
        copy.wait()
    gram[...] = tn(two[...], three[...])
    for i in range(0, leaves, 2):
        stacked = jnp.concatenate(projected[i : i + 2], axis=1)
        coef[:, i * rank : (i + 2) * rank] = exact_nt(stacked, cap[...]).astype(BF16)
    half = gram_keep.shape[0]
    _, me = place(bit)
    gram_keep[...] = gram[pl.ds(pl.multiple_of(me * half, half), half), :]
    gram_send[...] = gram[pl.ds(pl.multiple_of((1 - me) * half, half), half), :]


def local_kernel(leaf, bit, field, coef, one, two, three, field_out, send, keep, proj):
    m, n = field.shape
    leaves = n // leaf
    rank = one.shape[1]
    width = m // 4
    total = jnp.concatenate(
        [
            field[:, i * leaf : (i + 1) * leaf]
            - nt(coef[:, i * rank : (i + 1) * rank], one[pl.ds(i * leaf, leaf), :])
            for i in range(leaves)
        ],
        axis=1,
    )
    field_out[...] = total
    high, low = split(total, 2)
    proj[0] = nn(high, two[...])
    both = nn(jnp.concatenate([high, low], axis=0), three[...])
    proj[1] = both[:m] + both[m:]
    _, me = place(bit)
    for side in range(2):
        for level in range(2):
            for ref, core in ((keep, me), (send, 1 - me)):
                start = pl.multiple_of(side * 2 * width + core * width, width)
                ref[side, level] = proj[level, pl.ds(start, width), :]


def middle_kernel(
    bit, mine, other, cap, gram_own, gram_far, gram_swap, total_out, coef_own, coef_other, gram
):
    rank = mine.shape[2]
    half = rank // 2
    side, me = place(bit)
    here = pl.ds(pl.multiple_of(me * half, half), half)
    there = pl.ds(pl.multiple_of((1 - me) * half, half), half)
    for i, part in enumerate((gram_own, gram_far)):
        gram[i, here, :] = part[...]
        gram[i, there, :] = gram_swap[i]
    own, far = mine[0], other[0]
    is_first = side == 0
    stacked = jnp.concatenate(
        [jnp.where(is_first, own, far), jnp.where(is_first, far, own)], axis=1
    )
    coef = exact_nt(stacked, cap[...]).astype(BF16)
    left, right = coef[:, :rank].astype(F32), coef[:, rank:].astype(F32)
    c_own = jnp.where(is_first, left, right)
    c_far = jnp.where(is_first, right, left)
    coef_own[...] = c_own
    coef_other[...] = c_far
    total = mine[1] + other[1]
    for i, c in enumerate((c_own, c_far)):
        c = c.astype(BF16)
        for part in split(gram[i], 2):
            total = total - nn(c, part)
    total_out[...] = total


def last_coef_kernel(bit, mine, other, cap, out):
    rank = mine.shape[1]
    side = (lax.axis_index("row") >> bit) & 1
    is_first = side == 0
    own, far = mine[...], other[...]
    stacked = jnp.concatenate(
        [jnp.where(is_first, own, far), jnp.where(is_first, far, own)], axis=1
    )
    rows = cap[pl.ds(pl.multiple_of(side * rank, rank), rank), :]
    out[...] = exact_nt(stacked, rows).astype(BF16).astype(F32)


def gather_coef(bit, own, across, cores, scratch):
    width = own.shape[0]
    side, me = place(bit)

    def put(s, c, value):
        start = pl.multiple_of((s * 2 + c) * width, width)
        scratch[pl.ds(start, width), :] = value.astype(BF16)

    put(side, me, own[...])
    put(1 - side, me, across[...])
    put(side, 1 - me, cores[0])
    put(1 - side, 1 - me, cores[1])


def base_kernel(bit, field, own, across, cores, two, out, scratch):
    gather_coef(bit, own, across, cores, scratch)
    out[...] = jnp.transpose(field[...]) - nt(two[...], scratch[...])


def final_kernel(bit, base, own, across, cores, three, out_hbm, scratch, out, sems):
    gather_coef(bit, own, across, cores, scratch)
    chunks = sems.shape[0]
    size = out.shape[0] // chunks
    copies = []
    for i in range(chunks):
        rows = pl.ds(i * size, size)
        out[rows, :] = (base[rows, :] - nt(three[rows, :], scratch[...])).astype(BF16)
        copies.append(pltpu.make_async_copy(out.at[rows], out_hbm.at[rows], sems.at[i]))
        copies[-1].start()
    for copy in copies:
        copy.wait()


def share(own, across):
    return partner(jnp.stack([own, across]), "sub", 0)


def per_device(
    right_sides,
    leaf_inverse,
    basis_one,
    basis_two,
    basis_three,
    capacity_one,
    capacity_two,
    capacity_three,
):
    n, m = right_sides.shape
    leaf = leaf_inverse.shape[1]
    rank = basis_one.shape[1]
    leaves = n // leaf
    width = m // 4
    row_count = lax.axis_size("row")
    row_index = lax.axis_index("row")
    bit_two = (row_count // 8).bit_length() - 1
    bit_three = (row_count // 2).bit_length() - 1
    side = (row_index >> bit_two) & 1

    gram_send, gram_half, field, coef, two, three, one = pl.pallas_call(
        functools.partial(load_kernel, leaf, bit_two),
        out_shape=[
            jax.ShapeDtypeStruct((rank // 2, rank), F32),
            jax.ShapeDtypeStruct((rank // 2, rank), F32),
            jax.ShapeDtypeStruct((m, n), F32),
            jax.ShapeDtypeStruct((m, leaves * rank), BF16),
            jax.ShapeDtypeStruct((n, rank), BF16),
            jax.ShapeDtypeStruct((n, rank), BF16),
            jax.ShapeDtypeStruct((n, rank), BF16),
        ],
        in_specs=[pl.BlockSpec(memory_space=pltpu.HBM)] * 6,
        out_specs=[VM] * 7,
        scratch_shapes=[
            pltpu.VMEM(capacity_one.shape, BF16),
            pltpu.VMEM((n, m), BF16),
            pltpu.VMEM((n, leaf), BF16),
            pltpu.VMEM((rank, rank), F32),
            pltpu.SemaphoreType.DMA((2 * leaves + 4,)),
        ],
        compiler_params=params(12288),
        name="load",
    )(*(
        pltpu.with_memory_space_constraint(x, pltpu.HBM)
        for x in (right_sides, leaf_inverse, basis_two, basis_three, basis_one, capacity_one)
    ))
    gram_half = gram_half + partner(gram_send, "sub", 0)

    field, send, keep = pl.pallas_call(
        functools.partial(local_kernel, leaf, bit_two),
        out_shape=[
            jax.ShapeDtypeStruct((m, n), F32),
            jax.ShapeDtypeStruct((2, 2, width, rank), F32),
            jax.ShapeDtypeStruct((2, 2, width, rank), F32),
        ],
        in_specs=[VM] * 5,
        out_specs=[VM] * 3,
        scratch_shapes=[pltpu.VMEM((2, m, rank), F32)],
        compiler_params=params(8192),
        name="local",
    )(field, coef, one, two, three)

    both = keep + partner(send, "sub", 0)
    for bit in range(bit_two):
        both = both + partner(both, "row", bit)
        gram_half = gram_half + partner(gram_half, "row", bit)
    gram_far = across_chips(gram_half, bit_two)
    gram_swap = share(gram_half, gram_far)

    mine = lax.dynamic_index_in_dim(both, side, 0, keepdims=False)
    theirs = lax.dynamic_index_in_dim(both, 1 - side, 0, keepdims=False)
    other = across_chips(theirs, bit_two)
    piece = jax.ShapeDtypeStruct((width, rank), F32)
    total, two_own, two_far = pl.pallas_call(
        functools.partial(middle_kernel, bit_two),
        out_shape=[piece, piece, piece],
        in_specs=[VM] * 6,
        out_specs=[VM] * 3,
        scratch_shapes=[pltpu.VMEM((2, rank, rank), F32)],
        compiler_params=params(4096),
        name="middle",
    )(mine, other, capacity_two, gram_half, gram_far, gram_swap)

    for bit in range(bit_two + 1, bit_three):
        total = total + partner(total, "row", bit)
    sibling = partner(total, "row", bit_three)

    two_across = across_chips(two_far, bit_two)
    two_cores = share(two_own, two_across)
    base = pl.pallas_call(
        functools.partial(base_kernel, bit_two),
        out_shape=jax.ShapeDtypeStruct((n, m), F32),
        in_specs=[VM] * 5,
        out_specs=VM,
        scratch_shapes=[pltpu.VMEM((m, rank), BF16)],
        compiler_params=params(8192),
        name="base",
    )(field, two_own, two_across, two_cores, two)

    three_own = pl.pallas_call(
        functools.partial(last_coef_kernel, bit_three),
        out_shape=piece,
        in_specs=[VM] * 3,
        out_specs=VM,
        compiler_params=params(2048),
        name="last_coef",
    )(total, sibling, capacity_three)
    three_across = across_chips(three_own, bit_two)
    three_cores = share(three_own, three_across)
    return pl.pallas_call(
        functools.partial(final_kernel, bit_two),
        out_shape=jax.ShapeDtypeStruct((n, m), BF16),
        in_specs=[VM] * 5,
        out_specs=HB,
        scratch_shapes=[
            pltpu.VMEM((m, rank), BF16),
            pltpu.VMEM((n, m), BF16),
            pltpu.SemaphoreType.DMA((4,)),
        ],
        compiler_params=params(8192),
        name="final",
    )(base, three_own, three_across, three_cores, three)


def solution(mesh):
    rows = P(("grp", "row", "sub"), None)

    return jax.shard_map(
        per_device,
        mesh=mesh,
        in_specs=(rows,) * 5 + (P("grp", None),) * 3,
        out_specs=rows,
        check_vma=False,
    )
```

```python
import functools

import jax
import jax.numpy as jnp
from jax import lax
from jax.experimental import pallas as pl
from jax.experimental.pallas import tpu as pltpu
from jax.sharding import PartitionSpec as P


F32, BF16 = jnp.float32, jnp.bfloat16
VM = pl.BlockSpec(memory_space=pltpu.VMEM)
HB = pl.BlockSpec(memory_space=pl.ANY)


def nn(a, b):
    return lax.dot_general(a, b, (((1,), (0,)), ((), ())), preferred_element_type=F32)


def nt(a, b):
    return lax.dot_general(a, b, (((1,), (1,)), ((), ())), preferred_element_type=F32)


def tn(a, b):
    return lax.dot_general(a, b, (((0,), (0,)), ((), ())), preferred_element_type=F32)


def split(x, terms):
    parts = []
    for _ in range(terms - 1):
        part = x.astype(BF16)
        parts.append(part)
        x = x - part.astype(F32)
    parts.append(x.astype(BF16))
    return parts


def exact_nt(x, capacity):
    rows = x.shape[0]
    out = nt(jnp.concatenate(split(x, 2), axis=0), capacity)
    return out[:rows] + out[rows:]


def partner(array, axis, bit):
    return lax.ppermute(array, axis, [(i, i ^ 1 << bit) for i in range(lax.axis_size(axis))])


def across_chips(array, bit):
    cores = lax.axis_size("sub")
    mask = cores << bit | 1
    count = cores * lax.axis_size("row")
    return lax.ppermute(array, ("row", "sub"), [(i, i ^ mask) for i in range(count)])


def place(bit):
    side = (lax.axis_index("row") >> bit) & 1
    return side, lax.axis_index("sub") ^ side


def params(kib):
    return pltpu.CompilerParams(vmem_limit_bytes=kib * 1024)


def fetch(pairs, sems):
    copies = [
        pltpu.make_async_copy(src, dst, sems.at[i]) for i, (src, dst) in enumerate(pairs)
    ]
    for copy in copies:
        copy.start()
    return copies


def load_kernel(
    leaf, bit, rhs_hbm, inv_hbm, two_hbm, three_hbm, one_hbm, cap_hbm,
    gram_send, gram_keep, field, coef, two, three, one, cap, rhs, inv, gram, sems,
):
    n = rhs.shape[0]
    rank = one.shape[1]
    leaves = n // leaf
    pairs = []
    for i in range(leaves):
        rows = pl.ds(i * leaf, leaf)
        pairs.append((rhs_hbm.at[rows], rhs.at[rows]))
        pairs.append((inv_hbm.at[rows], inv.at[rows]))
    pairs += [(one_hbm, one), (two_hbm, two), (three_hbm, three), (cap_hbm, cap)]
    copies = fetch(pairs, sems)

    def solve(i):
        rows = pl.ds(i * leaf, leaf)
        field[:, i * leaf : (i + 1) * leaf] = nt(jnp.transpose(rhs[rows, :]), inv[rows, :])

    def onto_one(i):
        part = field[:, i * leaf : (i + 1) * leaf].astype(BF16)
        return nn(part, one[pl.ds(i * leaf, leaf), :])

    for copy in copies[:2]:
        copy.wait()
    solve(0)
    for copy in copies[2 : 2 * leaves + 1]:
        copy.wait()
    for i in range(1, leaves):
        solve(i)
    projected = [onto_one(i) for i in range(leaves)]
    for copy in copies[2 * leaves + 1 :]:
        copy.wait()
    gram[...] = tn(two[...], three[...])
    for i in range(0, leaves, 2):
        stacked = jnp.concatenate(projected[i : i + 2], axis=1)
        coef[:, i * rank : (i + 2) * rank] = exact_nt(stacked, cap[...]).astype(BF16)
    half = gram_keep.shape[0]
    _, me = place(bit)
    gram_keep[...] = gram[pl.ds(pl.multiple_of(me * half, half), half), :]
    gram_send[...] = gram[pl.ds(pl.multiple_of((1 - me) * half, half), half), :]


def local_kernel(leaf, bit, field, coef, one, two, three, field_out, send, keep, proj):
    m, n = field.shape
    leaves = n // leaf
    rank = one.shape[1]
    width = m // 4
    total = jnp.concatenate(
        [
            field[:, i * leaf : (i + 1) * leaf]
            - nt(coef[:, i * rank : (i + 1) * rank], one[pl.ds(i * leaf, leaf), :])
            for i in range(leaves)
        ],
        axis=1,
    )
    field_out[...] = total
    high, low = split(total, 2)
    proj[0] = nn(high, two[...])
    both = nn(jnp.concatenate([high, low], axis=0), three[...])
    proj[1] = both[:m] + both[m:]
    _, me = place(bit)
    for side in range(2):
        for level in range(2):
            for ref, core in ((keep, me), (send, 1 - me)):
                start = pl.multiple_of(core * 2 * width + side * width, width)
                ref[side, level] = proj[level, pl.ds(start, width), :]


def middle_kernel(
    bit, mine, other, cap, gram_own, gram_far, gram_swap, total_out, coef_own, coef_other, gram
):
    rank = mine.shape[2]
    half = rank // 2
    side, me = place(bit)
    here = pl.ds(pl.multiple_of(me * half, half), half)
    there = pl.ds(pl.multiple_of((1 - me) * half, half), half)
    for i, part in enumerate((gram_own, gram_far)):
        gram[i, here, :] = part[...]
        gram[i, there, :] = gram_swap[i]
    own, far = mine[0], other[0]
    is_first = side == 0
    stacked = jnp.concatenate(
        [jnp.where(is_first, own, far), jnp.where(is_first, far, own)], axis=1
    )
    coef = exact_nt(stacked, cap[...]).astype(BF16)
    left, right = coef[:, :rank].astype(F32), coef[:, rank:].astype(F32)
    c_own = jnp.where(is_first, left, right)
    c_far = jnp.where(is_first, right, left)
    coef_own[...] = c_own
    coef_other[...] = c_far
    total = mine[1] + other[1]
    for i, c in enumerate((c_own, c_far)):
        c = c.astype(BF16)
        for part in split(gram[i], 2):
            total = total - nn(c, part)
    total_out[...] = total


def last_coef_kernel(bit, mine, other, cap, out):
    rank = mine.shape[1]
    side = (lax.axis_index("row") >> bit) & 1
    is_first = side == 0
    own, far = mine[...], other[...]
    stacked = jnp.concatenate(
        [jnp.where(is_first, own, far), jnp.where(is_first, far, own)], axis=1
    )
    rows = cap[pl.ds(pl.multiple_of(side * rank, rank), rank), :]
    out[...] = exact_nt(stacked, rows).astype(BF16).astype(F32)


def gather_coef(bit, own, across, cores, scratch):
    width = own.shape[0]
    side, me = place(bit)

    def put(s, c, value):
        start = pl.multiple_of((c * 2 + s) * width, width)
        scratch[pl.ds(start, width), :] = value.astype(BF16)

    put(side, me, own[...])
    put(1 - side, me, across[...])
    put(side, 1 - me, cores[0])
    put(1 - side, 1 - me, cores[1])


def base_kernel(bit, field, own, across, cores, two, out, scratch):
    gather_coef(bit, own, across, cores, scratch)
    out[...] = jnp.transpose(field[...]) - nt(two[...], scratch[...])


def half_kernel(bit, base, own, across, three, out, scratch):
    width = own.shape[0]
    side, me = place(bit)
    scratch[pl.ds(pl.multiple_of(side * width, width), width), :] = own[...].astype(BF16)
    scratch[pl.ds(pl.multiple_of((1 - side) * width, width), width), :] = across[...].astype(BF16)
    columns = pl.ds(pl.multiple_of(me * 2 * width, 2 * width), 2 * width)
    out[...] = (base[:, columns] - nt(three[...], scratch[...])).astype(BF16)


def final_kernel(bit, base, half, cores, three, out_hbm, scratch, out, sems):
    width = cores.shape[1]
    side, me = place(bit)
    mine = pl.ds(pl.multiple_of(me * 2 * width, 2 * width), 2 * width)
    theirs = pl.ds(pl.multiple_of((1 - me) * 2 * width, 2 * width), 2 * width)
    copies = [pltpu.make_async_copy(half, out_hbm.at[:, mine], sems.at[0])]
    copies[0].start()
    for i in range(2):
        start = pl.multiple_of((side + i - 2 * side * i) * width, width)
        scratch[pl.ds(start, width), :] = cores[i].astype(BF16)
    chunks = sems.shape[0] - 1
    size = out.shape[0] // chunks
    for i in range(chunks):
        rows = pl.ds(i * size, size)
        out[rows, :] = (base[rows, theirs] - nt(three[rows, :], scratch[...])).astype(BF16)
        copies.append(pltpu.make_async_copy(out.at[rows], out_hbm.at[rows, theirs], sems.at[i + 1]))
        copies[-1].start()
    for copy in copies:
        copy.wait()


def share(own, across):
    return partner(jnp.stack([own, across]), "sub", 0)


def per_device(
    right_sides,
    leaf_inverse,
    basis_one,
    basis_two,
    basis_three,
    capacity_one,
    capacity_two,
    capacity_three,
):
    n, m = right_sides.shape
    leaf = leaf_inverse.shape[1]
    rank = basis_one.shape[1]
    leaves = n // leaf
    width = m // 4
    row_count = lax.axis_size("row")
    row_index = lax.axis_index("row")
    bit_two = (row_count // 8).bit_length() - 1
    bit_three = (row_count // 2).bit_length() - 1
    side = (row_index >> bit_two) & 1

    gram_send, gram_half, field, coef, two, three, one = pl.pallas_call(
        functools.partial(load_kernel, leaf, bit_two),
        out_shape=[
            jax.ShapeDtypeStruct((rank // 2, rank), F32),
            jax.ShapeDtypeStruct((rank // 2, rank), F32),
            jax.ShapeDtypeStruct((m, n), F32),
            jax.ShapeDtypeStruct((m, leaves * rank), BF16),
            jax.ShapeDtypeStruct((n, rank), BF16),
            jax.ShapeDtypeStruct((n, rank), BF16),
            jax.ShapeDtypeStruct((n, rank), BF16),
        ],
        in_specs=[pl.BlockSpec(memory_space=pltpu.HBM)] * 6,
        out_specs=[VM] * 7,
        scratch_shapes=[
            pltpu.VMEM(capacity_one.shape, BF16),
            pltpu.VMEM((n, m), BF16),
            pltpu.VMEM((n, leaf), BF16),
            pltpu.VMEM((rank, rank), F32),
            pltpu.SemaphoreType.DMA((2 * leaves + 4,)),
        ],
        compiler_params=params(12288),
        name="load",
    )(*(
        pltpu.with_memory_space_constraint(x, pltpu.HBM)
        for x in (right_sides, leaf_inverse, basis_two, basis_three, basis_one, capacity_one)
    ))
    gram_half = gram_half + partner(gram_send, "sub", 0)

    field, send, keep = pl.pallas_call(
        functools.partial(local_kernel, leaf, bit_two),
        out_shape=[
            jax.ShapeDtypeStruct((m, n), F32),
            jax.ShapeDtypeStruct((2, 2, width, rank), F32),
            jax.ShapeDtypeStruct((2, 2, width, rank), F32),
        ],
        in_specs=[VM] * 5,
        out_specs=[VM] * 3,
        scratch_shapes=[pltpu.VMEM((2, m, rank), F32)],
        compiler_params=params(8192),
        name="local",
    )(field, coef, one, two, three)

    both = keep + partner(send, "sub", 0)
    for bit in range(bit_two):
        both = both + partner(both, "row", bit)
        gram_half = gram_half + partner(gram_half, "row", bit)
    gram_far = across_chips(gram_half, bit_two)
    gram_swap = share(gram_half, gram_far)

    mine = lax.dynamic_index_in_dim(both, side, 0, keepdims=False)
    theirs = lax.dynamic_index_in_dim(both, 1 - side, 0, keepdims=False)
    other = across_chips(theirs, bit_two)
    piece = jax.ShapeDtypeStruct((width, rank), F32)
    total, two_own, two_far = pl.pallas_call(
        functools.partial(middle_kernel, bit_two),
        out_shape=[piece, piece, piece],
        in_specs=[VM] * 6,
        out_specs=[VM] * 3,
        scratch_shapes=[pltpu.VMEM((2, rank, rank), F32)],
        compiler_params=params(4096),
        name="middle",
    )(mine, other, capacity_two, gram_half, gram_far, gram_swap)

    for bit in range(bit_two + 1, bit_three):
        total = total + partner(total, "row", bit)
    sibling = partner(total, "row", bit_three)

    two_across = across_chips(two_far, bit_two)
    two_cores = share(two_own, two_across)
    base = pl.pallas_call(
        functools.partial(base_kernel, bit_two),
        out_shape=jax.ShapeDtypeStruct((n, m), F32),
        in_specs=[VM] * 5,
        out_specs=VM,
        scratch_shapes=[pltpu.VMEM((m, rank), BF16)],
        compiler_params=params(8192),
        name="base",
    )(field, two_own, two_across, two_cores, two)

    three_own = pl.pallas_call(
        functools.partial(last_coef_kernel, bit_three),
        out_shape=piece,
        in_specs=[VM] * 3,
        out_specs=VM,
        compiler_params=params(2048),
        name="last_coef",
    )(total, sibling, capacity_three)
    three_across = across_chips(three_own, bit_two)
    three_cores = share(three_own, three_across)
    half = pl.pallas_call(
        functools.partial(half_kernel, bit_two),
        out_shape=jax.ShapeDtypeStruct((n, 2 * width), BF16),
        in_specs=[VM] * 4,
        out_specs=VM,
        scratch_shapes=[pltpu.VMEM((2 * width, rank), BF16)],
        compiler_params=params(4096),
        name="half",
    )(base, three_own, three_across, three)
    return pl.pallas_call(
        functools.partial(final_kernel, bit_two),
        out_shape=jax.ShapeDtypeStruct((n, m), BF16),
        in_specs=[VM] * 4,
        out_specs=HB,
        scratch_shapes=[
            pltpu.VMEM((2 * width, rank), BF16),
            pltpu.VMEM((n, 2 * width), BF16),
            pltpu.SemaphoreType.DMA((3,)),
        ],
        compiler_params=params(8192),
        name="final",
    )(base, half, three_cores, three)


def solution(mesh):
    rows = P(("grp", "row", "sub"), None)

    return jax.shard_map(
        per_device,
        mesh=mesh,
        in_specs=(rows,) * 5 + (P("grp", None),) * 3,
        out_specs=rows,
        check_vma=False,
    )
```

```python
import functools

import jax
import jax.numpy as jnp
from jax import lax
from jax.experimental import pallas as pl
from jax.experimental.pallas import tpu as pltpu
from jax.sharding import PartitionSpec as P


F32, BF16 = jnp.float32, jnp.bfloat16
VM = pl.BlockSpec(memory_space=pltpu.VMEM)
HB = pl.BlockSpec(memory_space=pl.ANY)


def nn(a, b):
    return lax.dot_general(a, b, (((1,), (0,)), ((), ())), preferred_element_type=F32)


def nt(a, b):
    return lax.dot_general(a, b, (((1,), (1,)), ((), ())), preferred_element_type=F32)


def tn(a, b):
    return lax.dot_general(a, b, (((0,), (0,)), ((), ())), preferred_element_type=F32)


def split(x, terms):
    parts = []
    for _ in range(terms - 1):
        part = x.astype(BF16)
        parts.append(part)
        x = x - part.astype(F32)
    parts.append(x.astype(BF16))
    return parts


def exact_nt(x, capacity):
    rows = x.shape[0]
    out = nt(jnp.concatenate(split(x, 2), axis=0), capacity)
    return out[:rows] + out[rows:]


def partner(array, axis, bit):
    return lax.ppermute(array, axis, [(i, i ^ 1 << bit) for i in range(lax.axis_size(axis))])


def across_chips(array, bit):
    cores = lax.axis_size("sub")
    mask = cores << bit | 1
    count = cores * lax.axis_size("row")
    return lax.ppermute(array, ("row", "sub"), [(i, i ^ mask) for i in range(count)])


def place(bit):
    side = (lax.axis_index("row") >> bit) & 1
    return side, lax.axis_index("sub") ^ side


def params(kib):
    return pltpu.CompilerParams(vmem_limit_bytes=kib * 1024)


def fetch(pairs, sems):
    copies = [
        pltpu.make_async_copy(src, dst, sems.at[i]) for i, (src, dst) in enumerate(pairs)
    ]
    for copy in copies:
        copy.start()
    return copies


def load_kernel(
    leaf, bit, rhs_hbm, inv_hbm, two_hbm, three_hbm, one_hbm, cap_hbm,
    gram_send, gram_keep, field, coef, two, three, one, cap, rhs, inv, gram, sems,
):
    n = rhs.shape[0]
    rank = one.shape[1]
    leaves = n // leaf
    pairs = []
    for i in range(leaves):
        rows = pl.ds(i * leaf, leaf)
        pairs.append((rhs_hbm.at[rows], rhs.at[rows]))
        pairs.append((inv_hbm.at[rows], inv.at[rows]))
    pairs += [(one_hbm, one), (two_hbm, two), (three_hbm, three), (cap_hbm, cap)]
    copies = fetch(pairs, sems)

    def solve(i):
        rows = pl.ds(i * leaf, leaf)
        field[:, i * leaf : (i + 1) * leaf] = nt(jnp.transpose(rhs[rows, :]), inv[rows, :])

    def onto_one(i):
        part = field[:, i * leaf : (i + 1) * leaf].astype(BF16)
        return nn(part, one[pl.ds(i * leaf, leaf), :])

    copies[0].wait()
    first = jnp.transpose(rhs[pl.ds(0, leaf), :])
    copies[1].wait()
    field[:, :leaf] = nt(first, inv[pl.ds(0, leaf), :])
    for copy in copies[2 : 2 * leaves + 1]:
        copy.wait()
    for i in range(1, leaves):
        solve(i)
    projected = [onto_one(i) for i in range(leaves)]
    for copy in copies[2 * leaves + 1 :]:
        copy.wait()
    gram[...] = tn(two[...], three[...])
    for i in range(0, leaves, 2):
        stacked = jnp.concatenate(projected[i : i + 2], axis=1)
        coef[:, i * rank : (i + 2) * rank] = exact_nt(stacked, cap[...]).astype(BF16)
    half = gram_keep.shape[0]
    _, me = place(bit)
    gram_keep[...] = gram[pl.ds(pl.multiple_of(me * half, half), half), :]
    gram_send[...] = gram[pl.ds(pl.multiple_of((1 - me) * half, half), half), :]


def local_kernel(leaf, bit, field, coef, one, two, three, field_out, send, keep, proj):
    m, n = field.shape
    leaves = n // leaf
    rank = one.shape[1]
    width = m // 4
    total = jnp.concatenate(
        [
            field[:, i * leaf : (i + 1) * leaf]
            - nt(coef[:, i * rank : (i + 1) * rank], one[pl.ds(i * leaf, leaf), :])
            for i in range(leaves)
        ],
        axis=1,
    )
    field_out[...] = total
    high, low = split(total, 2)
    proj[0] = nn(high, two[...])
    both = nn(jnp.concatenate([high, low], axis=0), three[...])
    proj[1] = both[:m] + both[m:]
    _, me = place(bit)
    for side in range(2):
        for level in range(2):
            for ref, core in ((keep, me), (send, 1 - me)):
                start = pl.multiple_of(core * 2 * width + side * width, width)
                ref[side, level] = proj[level, pl.ds(start, width), :]


def middle_kernel(
    bit, mine, other, cap, gram_own, gram_far, gram_swap, total_out, coef_own, coef_other, gram
):
    rank = mine.shape[2]
    half = rank // 2
    side, me = place(bit)
    here = pl.ds(pl.multiple_of(me * half, half), half)
    there = pl.ds(pl.multiple_of((1 - me) * half, half), half)
    for i, part in enumerate((gram_own, gram_far)):
        gram[i, here, :] = part[...]
        gram[i, there, :] = gram_swap[i]
    own, far = mine[0], other[0]
    is_first = side == 0
    stacked = jnp.concatenate(
        [jnp.where(is_first, own, far), jnp.where(is_first, far, own)], axis=1
    )
    coef = exact_nt(stacked, cap[...]).astype(BF16)
    left, right = coef[:, :rank].astype(F32), coef[:, rank:].astype(F32)
    c_own = jnp.where(is_first, left, right)
    c_far = jnp.where(is_first, right, left)
    coef_own[...] = c_own
    coef_other[...] = c_far
    total = mine[1] + other[1]
    for i, c in enumerate((c_own, c_far)):
        c = c.astype(BF16)
        for part in split(gram[i], 2):
            total = total - nn(c, part)
    total_out[...] = total


def last_coef_kernel(bit, mine, other, cap, out):
    rank = mine.shape[1]
    side = (lax.axis_index("row") >> bit) & 1
    is_first = side == 0
    own, far = mine[...], other[...]
    stacked = jnp.concatenate(
        [jnp.where(is_first, own, far), jnp.where(is_first, far, own)], axis=1
    )
    rows = cap[pl.ds(pl.multiple_of(side * rank, rank), rank), :]
    out[...] = exact_nt(stacked, rows).astype(BF16).astype(F32)


def gather_coef(bit, own, across, cores, scratch):
    width = own.shape[0]
    side, me = place(bit)

    def put(s, c, value):
        start = pl.multiple_of((c * 2 + s) * width, width)
        scratch[pl.ds(start, width), :] = value.astype(BF16)

    put(side, me, own[...])
    put(1 - side, me, across[...])
    put(side, 1 - me, cores[0])
    put(1 - side, 1 - me, cores[1])


def base_kernel(bit, field, own, across, cores, two, out, scratch):
    gather_coef(bit, own, across, cores, scratch)
    out[...] = jnp.transpose(field[...]) - nt(two[...], scratch[...])


def half_kernel(bit, base, own, across, three, out, scratch):
    width = own.shape[0]
    side, me = place(bit)
    scratch[pl.ds(pl.multiple_of(side * width, width), width), :] = own[...].astype(BF16)
    scratch[pl.ds(pl.multiple_of((1 - side) * width, width), width), :] = across[...].astype(BF16)
    columns = pl.ds(pl.multiple_of(me * 2 * width, 2 * width), 2 * width)
    out[...] = (base[:, columns] - nt(three[...], scratch[...])).astype(BF16)


def final_kernel(bit, base, half, cores, three, out_hbm, scratch, out, sems):
    width = cores.shape[1]
    side, me = place(bit)
    mine = pl.ds(pl.multiple_of(me * 2 * width, 2 * width), 2 * width)
    theirs = pl.ds(pl.multiple_of((1 - me) * 2 * width, 2 * width), 2 * width)
    copies = [pltpu.make_async_copy(half, out_hbm.at[:, mine], sems.at[0])]
    copies[0].start()
    for i in range(2):
        start = pl.multiple_of((side + i - 2 * side * i) * width, width)
        scratch[pl.ds(start, width), :] = cores[i].astype(BF16)
    chunks = sems.shape[0] - 1
    size = out.shape[0] // chunks
    for i in range(chunks):
        rows = pl.ds(i * size, size)
        out[rows, :] = (base[rows, theirs] - nt(three[rows, :], scratch[...])).astype(BF16)
        copies.append(pltpu.make_async_copy(out.at[rows], out_hbm.at[rows, theirs], sems.at[i + 1]))
        copies[-1].start()
    for copy in copies:
        copy.wait()


def share(own, across):
    return partner(jnp.stack([own, across]), "sub", 0)


def per_device(
    right_sides,
    leaf_inverse,
    basis_one,
    basis_two,
    basis_three,
    capacity_one,
    capacity_two,
    capacity_three,
):
    n, m = right_sides.shape
    leaf = leaf_inverse.shape[1]
    rank = basis_one.shape[1]
    leaves = n // leaf
    width = m // 4
    row_count = lax.axis_size("row")
    row_index = lax.axis_index("row")
    bit_two = (row_count // 8).bit_length() - 1
    bit_three = (row_count // 2).bit_length() - 1
    side = (row_index >> bit_two) & 1

    gram_send, gram_half, field, coef, two, three, one = pl.pallas_call(
        functools.partial(load_kernel, leaf, bit_two),
        out_shape=[
            jax.ShapeDtypeStruct((rank // 2, rank), F32),
            jax.ShapeDtypeStruct((rank // 2, rank), F32),
            jax.ShapeDtypeStruct((m, n), F32),
            jax.ShapeDtypeStruct((m, leaves * rank), BF16),
            jax.ShapeDtypeStruct((n, rank), BF16),
            jax.ShapeDtypeStruct((n, rank), BF16),
            jax.ShapeDtypeStruct((n, rank), BF16),
        ],
        in_specs=[pl.BlockSpec(memory_space=pltpu.HBM)] * 6,
        out_specs=[VM] * 7,
        scratch_shapes=[
            pltpu.VMEM(capacity_one.shape, BF16),
            pltpu.VMEM((n, m), BF16),
            pltpu.VMEM((n, leaf), BF16),
            pltpu.VMEM((rank, rank), F32),
            pltpu.SemaphoreType.DMA((2 * leaves + 4,)),
        ],
        compiler_params=params(12288),
        name="load",
    )(*(
        pltpu.with_memory_space_constraint(x, pltpu.HBM)
        for x in (right_sides, leaf_inverse, basis_two, basis_three, basis_one, capacity_one)
    ))
    gram_half = gram_half + partner(gram_send, "sub", 0)

    field, send, keep = pl.pallas_call(
        functools.partial(local_kernel, leaf, bit_two),
        out_shape=[
            jax.ShapeDtypeStruct((m, n), F32),
            jax.ShapeDtypeStruct((2, 2, width, rank), F32),
            jax.ShapeDtypeStruct((2, 2, width, rank), F32),
        ],
        in_specs=[VM] * 5,
        out_specs=[VM] * 3,
        scratch_shapes=[pltpu.VMEM((2, m, rank), F32)],
        compiler_params=params(8192),
        name="local",
    )(field, coef, one, two, three)

    both = keep + partner(send, "sub", 0)
    for bit in range(bit_two):
        both = both + partner(both, "row", bit)
        gram_half = gram_half + partner(gram_half, "row", bit)
    gram_far = across_chips(gram_half, bit_two)
    gram_swap = share(gram_half, gram_far)

    mine = lax.dynamic_index_in_dim(both, side, 0, keepdims=False)
    theirs = lax.dynamic_index_in_dim(both, 1 - side, 0, keepdims=False)
    other = across_chips(theirs, bit_two)
    piece = jax.ShapeDtypeStruct((width, rank), F32)
    total, two_own, two_far = pl.pallas_call(
        functools.partial(middle_kernel, bit_two),
        out_shape=[piece, piece, piece],
        in_specs=[VM] * 6,
        out_specs=[VM] * 3,
        scratch_shapes=[pltpu.VMEM((2, rank, rank), F32)],
        compiler_params=params(4096),
        name="middle",
    )(mine, other, capacity_two, gram_half, gram_far, gram_swap)

    for bit in range(bit_two + 1, bit_three):
        total = total + partner(total, "row", bit)
    sibling = partner(total, "row", bit_three)

    two_across = across_chips(two_far, bit_two)
    two_cores = share(two_own, two_across)
    base = pl.pallas_call(
        functools.partial(base_kernel, bit_two),
        out_shape=jax.ShapeDtypeStruct((n, m), F32),
        in_specs=[VM] * 5,
        out_specs=VM,
        scratch_shapes=[pltpu.VMEM((m, rank), BF16)],
        compiler_params=params(8192),
        name="base",
    )(field, two_own, two_across, two_cores, two)

    three_own = pl.pallas_call(
        functools.partial(last_coef_kernel, bit_three),
        out_shape=piece,
        in_specs=[VM] * 3,
        out_specs=VM,
        compiler_params=params(2048),
        name="last_coef",
    )(total, sibling, capacity_three)
    three_across = across_chips(three_own, bit_two)
    three_cores = share(three_own, three_across)
    half = pl.pallas_call(
        functools.partial(half_kernel, bit_two),
        out_shape=jax.ShapeDtypeStruct((n, 2 * width), BF16),
        in_specs=[VM] * 4,
        out_specs=VM,
        scratch_shapes=[pltpu.VMEM((2 * width, rank), BF16)],
        compiler_params=params(4096),
        name="half",
    )(base, three_own, three_across, three)
    return pl.pallas_call(
        functools.partial(final_kernel, bit_two),
        out_shape=jax.ShapeDtypeStruct((n, m), BF16),
        in_specs=[VM] * 4,
        out_specs=HB,
        scratch_shapes=[
            pltpu.VMEM((2 * width, rank), BF16),
            pltpu.VMEM((n, 2 * width), BF16),
            pltpu.SemaphoreType.DMA((3,)),
        ],
        compiler_params=params(8192),
        name="final",
    )(base, half, three_cores, three)


def solution(mesh):
    rows = P(("grp", "row", "sub"), None)

    return jax.shard_map(
        per_device,
        mesh=mesh,
        in_specs=(rows,) * 5 + (P("grp", None),) * 3,
        out_specs=rows,
        check_vma=False,
    )
```
